1024 devices in a mesh: pipe: 8 (over y, core), expert: 32 (over z), dp: 4 (over x).
Axes of the slice: x: 4, y: 4, z: 32, core: 2. Of those that a mesh axis runs over, the one named last changes fastest.
Arguments:
- section_grad: bfloat16 [8, 16384, 7168], P('pipe', ('expert', 'dp')), may hold values from -6 to 6
- loss_grad: bfloat16 [16384, 7168], P(('expert', 'dp')), may hold values from -6 to 6
- expert_ids: int32 [8, 16384, 8], P('pipe', ('expert', 'dp')), may hold values from 0 to 255, all different within a row
- gate_values: bfloat16 [8, 16384, 8], P('pipe', ('expert', 'dp')), may hold values from 0.049804688 to 0.59765625
- down_inputs: bfloat16 [8, 4, 128, 8192], P('pipe', 'dp', None, 'expert'), may hold values from -1.59375 to 1.59375
Outputs:
- down_grad: bfloat16 [8, 7168, 8192], P('pipe', 'dp', 'expert')
The draws below stay inside these ranges and needn't reach their ends.
Inputs may be any that keep to these rules, and one draw needn't show every extreme that they name: `expert_ids`: each row names 8 different experts; every expert is named by some row.
All inputs are finite; a program needn't handle non-finite values.
Results may differ from the reference program's by a relative error of at most 0.009.
Values may be sent and summed in bfloat16 or wider, within the bound.
No kernel may reach another device: no remote copies, remote signals or barrier semaphores. Data moves between devices by JAX's collectives and lax.ppermute only.
A program may use at most 32 MiB of HBM per device.

```python
import jax
import jax.numpy as jnp
from jax import lax

D = 7168
ROUTED = 256
TOPK = 8
HID = 1024
TOK_DEV = 128
CAP = 4
EXPERTS = 8
GROUPS = 4
SECTIONS = 8
TOKENS = 16384
SLOTS = 128


def shard_levels(key, extent, split, least, top_value):
    factor_of, own = 1.0, jax.random.fold_in(key, 6)
    for position, blocks in split:
        heights = jnp.exp(jax.random.uniform(jax.random.fold_in(own, position), (blocks,), jnp.float32, least / len(split), top_value / len(split)))
        factor_of = factor_of * jnp.repeat(heights, extent[position] // blocks).reshape([-1 if axis == position else 1 for axis in range(len(extent))])
    return factor_of


def choose_distinct(stream_key, rows, amount, top, lift):
    sequence = jax.random.permutation(jax.random.fold_in(stream_key, 1), amount)
    boost = sequence
    for power in range(3):
        boost = boost * boost // amount
    boost = boost * lift // amount
    tickets = jax.random.randint(jax.random.fold_in(stream_key, 2), (rows, amount), 0, 4096) + boost
    holders = jax.random.permutation(jax.random.fold_in(stream_key, 3), rows)[jnp.arange(amount) % rows]
    tickets = jnp.where(jnp.arange(rows)[:, None] == holders[None, :], 1 << 14, tickets)
    score = tickets * amount + jnp.arange(amount)
    return lax.top_k(score.astype(jnp.int32), top)[1].astype(jnp.int32)


def bell_draw(stream_key, dims, scale, reach, shards=(), kind=jnp.bfloat16):
    gain = shard_levels(stream_key, dims, shards, -0.22, 0.18) if shards else 1.0
    drawn = jax.random.normal(stream_key, dims, jnp.float32) * scale * gain
    return jnp.minimum(jnp.maximum(drawn, -reach), reach).astype(kind)


def setup_inputs(seed: int = 0) -> dict:
    splits = jax.random.split(jax.random.key(seed), 6)
    return {
        "section_grad": bell_draw(splits[0], (SECTIONS, TOKENS, D), 1.0, 6.0, ((0, 8), (1, 128))),
        "loss_grad": bell_draw(splits[1], (TOKENS, D), 1.0, 6.0, ((0, 128),)),
        "expert_ids": choose_distinct(splits[2], SECTIONS * TOKENS, ROUTED, TOPK, 512).reshape((SECTIONS, TOKENS, TOPK)),
        "gate_values": jnp.clip(0.049804688 + 0.54785156 * jax.random.uniform(splits[3], (SECTIONS, TOKENS, TOPK), jnp.float32) ** shard_levels(splits[3], (SECTIONS, TOKENS, TOPK), ((0, 8), (1, 128)), -0.2, 0.2), 0.049804688, 0.59765625).astype(jnp.bfloat16),
        "down_inputs": bell_draw(splits[4], (SECTIONS, GROUPS, SLOTS, EXPERTS * HID), 0.2, 1.59375, ((0, 8), (1, 4), (3, 32))),
    }


def route_tables(id_table, gate_table):
    n_blocks = id_table.shape[0] // TOK_DEV
    flat_ids = id_table.reshape(n_blocks, TOK_DEV * TOPK)
    onehot = (flat_ids[:, :, None] == jnp.arange(EXPERTS, dtype=jnp.int32)[None, None, :]).astype(jnp.int32)
    before = jnp.cumsum(onehot, axis=1) - onehot
    ranks = jnp.sum(before * onehot, axis=2)
    retained = (flat_ids < EXPERTS) & (ranks < CAP)
    blocks = jnp.arange(n_blocks, dtype=jnp.int32)[:, None]
    source = blocks // GROUPS
    member = blocks % GROUPS
    overall = GROUPS * EXPERTS * SLOTS
    target = (member * EXPERTS + flat_ids) * SLOTS + source * CAP + ranks
    target = jnp.where(retained, target, overall).reshape(-1).astype(jnp.int32)
    routes = jnp.arange(TOK_DEV * TOPK, dtype=jnp.int32)[None, :]
    tokens = (blocks * TOK_DEV + routes // TOPK).reshape(-1).astype(jnp.int32)
    token_of = jnp.zeros((overall + 1,), jnp.int32).at[target].set(tokens)
    gate_of = jnp.zeros((overall + 1,), jnp.float32).at[target].set(gate_table.reshape(-1).astype(jnp.float32))
    return token_of[:overall], gate_of[:overall]


def section_weights(upstream, id_table, gate_table, inputs_section):
    token_of, gate_of = route_tables(id_table, gate_table)
    scaled = (jnp.take(upstream, token_of, axis=0).astype(jnp.float32) * gate_of[:, None]).astype(jnp.bfloat16)
    scaled = scaled.reshape(GROUPS, EXPERTS, SLOTS, D)
    accumulated = jnp.zeros((EXPERTS, D, HID), jnp.float32)
    for member in range(GROUPS):
        inputs_now = inputs_section[member].reshape(SLOTS, EXPERTS, HID).astype(jnp.float32)
        partial_value = jnp.einsum("esd,seh->edh", scaled[member].astype(jnp.float32), inputs_now)
        rounded = lax.optimization_barrier(partial_value.astype(jnp.bfloat16))
        accumulated = accumulated + rounded.astype(jnp.float32)
    result = accumulated.astype(jnp.bfloat16)
    return jnp.transpose(result, (1, 0, 2)).reshape(D, EXPERTS * HID)


def reference(section_grad, loss_grad, expert_ids, gate_values, down_inputs):
    results = []
    for section_index in range(SECTIONS):
        if section_index + 1 < SECTIONS:
            upstream = section_grad[section_index + 1]
        else:
            upstream = loss_grad
        results.append(section_weights(upstream, expert_ids[section_index], gate_values[section_index], down_inputs[section_index]))
    return jnp.stack(results, axis=0)
```

```python
import jax
import jax.numpy as jnp
from jax import lax
from jax.experimental import pallas as pl
from jax.experimental.pallas import tpu as pltpu
from jax.sharding import PartitionSpec as P

ROUTED = 256
TOPK = 8
SPLIT = 4
LANES = 128
HALF = 64
VMEM = pltpu.MemorySpace.VMEM
SMEM = pltpu.MemorySpace.SMEM


def select_kernel(ids_ref, gates_ref, out_ref):
    rows, tokens = out_ref.shape
    experts = rows // 4
    ids = ids_ref[0]
    gates = gates_ref[0].astype(jnp.float32)
    row = lax.broadcasted_iota(jnp.int32, (tokens, tokens), 1)
    expert = jnp.where(row < rows, (row >> 1) % experts, -1)
    slot = 2 * (row // (2 * experts)) + (row & 1)
    hit = jnp.zeros((tokens, tokens), jnp.float32)
    gate = jnp.zeros((tokens, tokens), jnp.float32)
    for k in range(ids.shape[1]):
        match = ids[:, k : k + 1] == expert
        hit = jnp.where(match, 1.0, hit)
        gate = jnp.where(match, gates[:, k : k + 1], gate)
    token = lax.broadcasted_iota(jnp.int32, (tokens, tokens), 0)
    earlier = jnp.where(row < token, 1.0, 0.0).astype(jnp.bfloat16)
    rank = jnp.dot(earlier, hit.astype(jnp.bfloat16), preferred_element_type=jnp.float32)
    chosen = jnp.where((hit > 0.0) & (rank == slot.astype(jnp.float32)), gate, 0.0)
    out_ref[...] = chosen.T[:rows].astype(jnp.bfloat16)


def compact_kernel(selector_ref, rows_ref, out_ref):
    quarters, subs, lines, width = out_ref.shape
    lane = lax.broadcasted_iota(jnp.int32, (lines, LANES), 1)
    low = lane < HALF
    selector = selector_ref[...]
    for d in range(quarters):
        for u in range(subs // 2):
            begin = (d * (subs // 2) + u) * width
            found = jnp.dot(selector, rows_ref[:, begin : begin + width], preferred_element_type=jnp.float32)
            for t in range(width // LANES):
                first = found[:lines, t * LANES : (t + 1) * LANES]
                second = found[lines:, t * LANES : (t + 1) * LANES]
                left = jnp.where(low, first, pltpu.roll(second, HALF, 1))
                right = jnp.where(low, pltpu.roll(first, HALF, 1), second)
                out_ref[d, 2 * u, :, t * LANES : (t + 1) * LANES] = left.astype(jnp.bfloat16)
                out_ref[d, 2 * u + 1, :, t * LANES : (t + 1) * LANES] = right.astype(jnp.bfloat16)


def product_kernel(place_ref, slots_ref, near_ref, far_ref, *out_refs):
    groups, lines, width = slots_ref.shape
    own = place_ref[0]
    slots = jnp.concatenate([slots_ref[own ^ j] for j in range(groups)], axis=0)
    turned = slots.astype(jnp.float32).T.astype(jnp.bfloat16)
    tiles = width // LANES
    parts = [
        jnp.concatenate([turned[t * LANES + h * HALF : t * LANES + (h + 1) * HALF] for t in range(tiles)], axis=0)
        for h in range(2)
    ]
    for i, out_ref in enumerate(out_refs):
        total = None
        for h in range(2):
            weights = jnp.concatenate(
                [near_ref[0, i, h], near_ref[1, i, h], far_ref[0, i, h], far_ref[1, i, h]], axis=0
            )
            term = jnp.dot(parts[h], weights, preferred_element_type=jnp.float32)
            total = term if total is None else total + term
        out_ref[...] = total.astype(jnp.bfloat16).reshape(out_ref.shape)


def place_kernel(place_ref, *refs):
    out_ref = refs[-1]
    own = place_ref[0]
    for i, block_ref in enumerate(refs[:-1]):
        member = own ^ i
        out_ref[member >> 1, :, member & 1] = block_ref[...]


def call(kernel, out_shapes, operands, scalars=0):
    specs = [pl.BlockSpec(memory_space=SMEM if n < scalars else VMEM) for n in range(len(operands))]
    single = not isinstance(out_shapes, list)
    shapes = [out_shapes] if single else out_shapes
    out = pl.pallas_call(
        kernel,
        in_specs=specs,
        out_specs=[pl.BlockSpec(memory_space=VMEM) for _ in shapes],
        out_shape=[jax.ShapeDtypeStruct(shape, jnp.bfloat16) for shape in shapes],
        name=kernel.__name__,
    )(*operands)
    return out[0] if single else out


def shift(value, axis, steps):
    count = lax.axis_size(axis)
    return lax.ppermute(value, axis, [(n, (n + steps) % count) for n in range(count)])


def swap(value, axis, mask):
    return lax.ppermute(value, axis, [(n, n ^ mask) for n in range(lax.axis_size(axis))])


def local(section_grad, loss_grad, expert_ids, gate_values, down_inputs):
    expert_count = lax.axis_size("expert")
    groups = lax.axis_size("dp")
    experts = expert_count // SPLIT
    tokens = section_grad.shape[1]
    model_width = section_grad.shape[2]
    columns = down_inputs.shape[3]
    capacity = tokens * TOPK // ROUTED
    width = model_width // (2 * groups)
    tiles = width // LANES

    selector = call(select_kernel, (experts * capacity, tokens), (expert_ids, gate_values))
    selector = shift(selector, "pipe", 1)
    first = lax.axis_index("pipe") == 0
    upstream = jnp.where(first, loss_grad, section_grad[0])
    picked = call(compact_kernel, (groups, SPLIT, experts * 2, width), (selector, upstream))
    picked = shift(picked, "pipe", -1)
    outgoing = picked.reshape(groups, SPLIT, experts, 2, width).transpose(0, 2, 1, 3, 4)
    outgoing = outgoing.reshape(groups * expert_count, 2, width)
    arrived = lax.all_to_all(outgoing, ("dp", "expert"), split_axis=0, concat_axis=0, tiled=True)
    slots = arrived.reshape(groups, expert_count * 2, width)

    saved = down_inputs[0, 0].reshape(expert_count, 2, 2, columns).transpose(1, 0, 2, 3)
    saved = saved.reshape(1, 2, expert_count * 2, columns)
    saved = jnp.concatenate([saved, swap(saved, "expert", 1)], axis=0)
    saved = jnp.concatenate([saved, swap(saved, "expert", 2)], axis=0)[None]
    near = jnp.concatenate([saved, swap(saved, "dp", 1)], axis=0)
    far = swap(near, "dp", 2)

    block = (tiles, HALF, columns)
    terms = call(
        product_kernel, [block] * SPLIT, (lax.axis_index("dp").reshape(1), slots, near, far), scalars=1
    )
    blocks = [terms[0]] + [swap(terms[i], "expert", i) for i in range(1, SPLIT)]
    member = (lax.axis_index("expert") % SPLIT).reshape(1)
    out = call(place_kernel, (2, tiles, 2, HALF, columns), (member, *blocks), scalars=1)
    return out.reshape(1, 2 * width, columns)


def solution(mesh):
    in_specs = (
        P("pipe", ("expert", "dp"), None),
        P(("expert", "dp"), None),
        P("pipe", ("expert", "dp"), None),
        P("pipe", ("expert", "dp"), None),
        P("pipe", "dp", None, "expert"),
    )
    out_specs = P("pipe", "dp", "expert")
    return jax.shard_map(local, mesh=mesh, in_specs=in_specs, out_specs=out_specs, check_vma=False)
```
